32 devices in a mesh: section: 4 (over y, core), chan: 8 (over z, x).
Axes of the slice: x: 2, y: 2, z: 4, core: 2. Of those that a mesh axis runs over, the one named last changes fastest.
Arguments:
- raw_traces: bfloat16 [2048, 1024], P(('section', 'chan')), may hold values from -6 to 6
- fir_taps: bfloat16 [64], replicated, may hold values from -0.75 to 0.75
- space_taps: float32 [33], replicated, may hold values from -1 to 1
- source_index: int32 [4, 96], P('section', 'chan'), may hold values from 0 to 511, as said below
Outputs:
- gathers: bfloat16 [2048, 64, 96], P(('section', 'chan'))
The draws below stay inside these ranges and needn't reach their ends.
Inputs may be any that keep to these rules, and one draw needn't show every extreme that they name: `source_index`: entries j * 12 to (j + 1) * 12 - 1 of a section's row are distinct and lie in channels j * 64 to (j + 1) * 64 - 1; the first such block of every section names channel 0 and the last names channel 512 - 1.
All inputs are finite; a program needn't handle non-finite values.
Results may differ from the reference program's by a relative error of at most 0.0058.
Values may be sent and summed in bfloat16 or wider, within the bound.
A program may use at most 64 MiB of HBM per device.

```python
import jax
import jax.numpy as jnp
from jax import lax

CH_DEV = 64
NT = 1024
KT = 64
SK = 33
LAGS = 64
SRC_DEV = 12
SRC = 96
SEC_CH = 512
CHANNELS = 2048


def draw_source_index(key, part):
    nchan = SRC // SRC_DEV
    nsect = CHANNELS // SEC_CH
    blocks = nsect * nchan
    keys = jax.random.split(key, blocks)
    picks = jax.vmap(lambda k: jax.random.permutation(k, CH_DEV)[:SRC_DEV])(keys).astype(jnp.int32)
    where_block = jnp.arange(blocks, dtype=jnp.int32) % nchan
    has_first = jnp.any(picks == 0, axis=1)
    has_last = jnp.any(picks == CH_DEV - 1, axis=1)
    set_first = (where_block == 0) & jnp.logical_not(has_first)
    set_last = (where_block == nchan - 1) & jnp.logical_not(has_last)
    column = jnp.arange(SRC_DEV, dtype=jnp.int32)[None, :] == 0
    picks = jnp.where(set_first[:, None] & column, 0, picks)
    picks = jnp.where(set_last[:, None] & column, CH_DEV - 1, picks)
    values = picks + (where_block * CH_DEV)[:, None]
    return values.reshape(nsect, SRC).astype(jnp.int32)


def block_scale(own_key, shape, cuts, smallest, top_value):
    def one(position, parts):
        heights = jax.random.uniform(jax.random.fold_in(jax.random.fold_in(own_key, 6), position), (parts,), jnp.float32, smallest / len(cuts), top_value / len(cuts))
        return jnp.repeat(jnp.exp(heights), shape[position] // parts).reshape((-1,) + (1,) * (len(shape) - position - 1))

    gain = one(*cuts[0])
    for cut in cuts[1:]:
        gain = gain * one(*cut)
    return gain


def centred(key, shape, spread, limit, shards=(), held_as=jnp.bfloat16):
    gain = block_scale(key, shape, shards, -0.22, 0.18) if shards else 1.0
    entries = jax.random.normal(key, shape, jnp.float32) * spread * gain
    return jnp.minimum(jnp.maximum(entries, -limit), limit).astype(held_as)


def setup_inputs(seed: int = 0) -> dict:
    seeds = jax.random.split(jax.random.key(seed), 5)
    return {
        "raw_traces": centred(seeds[0], (CHANNELS, NT), 1.0, 6.0, ((0, 32),)),
        "fir_taps": centred(seeds[1], (KT,), KT ** -0.5, 0.75),
        "space_taps": centred(seeds[2], (SK,), SK ** -0.5, 1.0, (), jnp.float32),
        "source_index": draw_source_index(jax.random.fold_in(seeds[4], 71), 0),
    }


def fir_matrix(taps, length):
    count = taps.shape[0]
    lead = jnp.zeros((length - 1,), taps.dtype)
    tail = jnp.zeros((length + 1 - count,), taps.dtype)
    period = jnp.concatenate([lead, taps, tail])
    flat = jnp.tile(period, length)[: length * (2 * length - 1)]
    return flat.reshape(length, 2 * length - 1)[:, length - 1:]


def space_filter(padded, space_taps, rows):
    total = jnp.zeros((rows, padded.shape[1]), jnp.float32)
    for offset in range(space_taps.shape[0]):
        total = total + space_taps[offset] * padded[offset:offset + rows].astype(jnp.float32)
    return total.astype(jnp.bfloat16)


def correlate(receivers, sources):
    rows, length = receivers.shape
    blocks = []
    for first in range(0, LAGS, 8):
        shifted = []
        for lag in range(first, first + 8):
            shifted.append(jnp.pad(receivers[:, lag:], ((0, 0), (0, lag))))
        stacked = jnp.stack(shifted, axis=1).reshape(rows * 8, length)
        block = lax.dot_general(stacked, sources, (((1,), (1,)), ((), ())), preferred_element_type=jnp.float32)
        blocks.append(block.reshape(rows, 8, sources.shape[0]))
    joined = jnp.concatenate(blocks, axis=1)
    return (joined * (1.0 / (length ** 0.5))).astype(jnp.bfloat16)


def reference(raw_traces, fir_taps, space_taps, source_index):
    length = raw_traces.shape[1]
    banded = jnp.dot(raw_traces, fir_matrix(fir_taps, length), preferred_element_type=jnp.float32).astype(jnp.bfloat16)
    half = (space_taps.shape[0] - 1) // 2
    padded = jnp.pad(banded, ((half, half), (0, 0)))
    filtered = space_filter(padded, space_taps, banded.shape[0])

    def one_section(sect):
        block = lax.dynamic_slice_in_dim(filtered, (sect * SEC_CH).astype(jnp.int32), SEC_CH, 0)
        sources = jnp.take(block, source_index[sect], axis=0)
        return correlate(block, sources)

    result = lax.map(one_section, jnp.arange(source_index.shape[0], dtype=jnp.int32))
    return result.reshape(raw_traces.shape[0], LAGS, source_index.shape[1])
```

```python
import functools

import jax
import jax.numpy as jnp
from jax import lax
from jax.experimental import pallas as pl
from jax.experimental.pallas import tpu as pltpu
from jax.sharding import PartitionSpec as P

LAGS = 64
MINOR = 8
SLOT = 16
LANES = 128
F32, BF16 = jnp.float32, jnp.bfloat16


def iota(shape, dim):
    return lax.broadcasted_iota(jnp.int32, shape, dim)


def dot(a, b, contract=((1,), (0,))):
    return lax.dot_general(a, b, (contract, ((), ())), preferred_element_type=F32)


def fir_block(fir_ref, line_ref):
    taps = fir_ref.shape[1]
    line_ref[...] = jnp.zeros(line_ref.shape, F32)
    line_ref[0:1, 0:taps] = fir_ref[...].astype(F32)
    wide = jnp.broadcast_to(line_ref[0:1, 0 : 2 * LANES], (2 * LANES, 2 * LANES))
    toeplitz = pltpu.roll(wide, LANES, 1, stride=1, stride_axis=0)[:, :LANES]
    flip = (iota((LANES, LANES), 0) + iota((LANES, LANES), 1) == LANES - 1).astype(F32)
    return dot(toeplitz.astype(BF16), flip.astype(BF16)).astype(BF16)


def fir(x, block, out_ref, first):
    rows, length = x.shape
    count = length // LANES
    parts = []
    for b in range(count):
        now = x[:, b * LANES : (b + 1) * LANES]
        before = x[:, (b - 1) * LANES : b * LANES] if b else jnp.zeros_like(now)
        parts.append(jnp.concatenate([before, now], axis=1))
    y = dot(jnp.concatenate(parts, axis=0), block).astype(BF16)
    for b in range(count):
        at = (count - 1 - b) * LANES
        out_ref[first : first + rows, at : at + LANES] = y[b * rows : (b + 1) * rows]


def split3(x):
    high = x.astype(BF16)
    rest = x - high.astype(F32)
    middle = rest.astype(BF16)
    low = (rest - middle.astype(F32)).astype(BF16)
    return high, middle, low


def exchange_kernel(
    sections, chans,
    index_ref, space_ref, fir_ref, raw_ref,
    gathered_ref, shifted_ref,
    line, band, halo, send, slots, halo_send, halo_recv, send_sem, recv_sem,
):
    rows, length = raw_ref.shape
    half = halo.shape[0] // 2
    sec, ch = lax.axis_index("section"), lax.axis_index("chan")
    me = sec * chans + ch
    last = sections * chans - 1
    has_prev, has_next = me > 0, me < last
    prev = jnp.maximum(me - 1, 0)
    after = jnp.minimum(me + 1, last)
    prev_id = (prev // chans, prev % chans)
    next_id = (after // chans, after % chans)

    barrier = pltpu.get_barrier_semaphore()
    for k in range(1, chans):
        pl.semaphore_signal(
            barrier, inc=1, device_id=(sec, (ch + k) % chans),
            device_id_type=pl.DeviceIdType.MESH,
        )
    cross_prev = jnp.logical_and(ch == 0, has_prev)
    cross_next = jnp.logical_and(ch == chans - 1, has_next)

    @pl.when(cross_prev)
    def _():
        pl.semaphore_signal(barrier, inc=1, device_id=prev_id, device_id_type=pl.DeviceIdType.MESH)

    @pl.when(cross_next)
    def _():
        pl.semaphore_signal(barrier, inc=1, device_id=next_id, device_id_type=pl.DeviceIdType.MESH)

    pl.semaphore_wait(
        barrier, chans - 1 + cross_prev.astype(jnp.int32) + cross_next.astype(jnp.int32)
    )

    to_next = pltpu.make_async_remote_copy(
        src_ref=raw_ref.at[rows - half : rows], dst_ref=halo.at[0:half],
        send_sem=halo_send.at[0], recv_sem=halo_recv.at[0],
        device_id=next_id, device_id_type=pl.DeviceIdType.MESH,
    )
    to_prev = pltpu.make_async_remote_copy(
        src_ref=raw_ref.at[0:half], dst_ref=halo.at[half : 2 * half],
        send_sem=halo_send.at[1], recv_sem=halo_recv.at[1],
        device_id=prev_id, device_id_type=pl.DeviceIdType.MESH,
    )

    @pl.when(has_next)
    def _():
        to_next.start()

    @pl.when(has_prev)
    def _():
        to_prev.start()

    block = fir_block(fir_ref, line)
    fir(raw_ref[...], block, band, half)

    taps = space_ref.shape[0]
    spread = rows + 2 * half
    offset = iota((rows, spread), 1) - iota((rows, spread), 0)
    mix = jnp.zeros((rows, spread), F32)
    for j in range(taps):
        mix = jnp.where(offset == j, space_ref[j], mix)
    mix = jnp.concatenate(split3(mix), axis=1)
    count = index_ref.shape[1]
    row, col = iota((SLOT, rows), 0), iota((SLOT, rows), 1)
    pick = jnp.zeros((SLOT, rows), F32)
    for i in range(count):
        chosen = jnp.logical_and(row == i, col == index_ref[0, i] - ch * rows)
        pick = jnp.where(chosen, 1.0, pick)
    source_mix = dot(pick.astype(BF16), mix).astype(BF16)

    @pl.when(has_next)
    def _():
        to_next.wait_send()

    @pl.when(has_prev)
    def _():
        to_prev.wait_send()

    @pl.when(has_prev)
    def _():
        to_next.wait_recv()

    @pl.when(jnp.logical_not(has_prev))
    def _():
        halo[0:half] = jnp.zeros((half, length), BF16)

    @pl.when(has_next)
    def _():
        to_prev.wait_recv()

    @pl.when(jnp.logical_not(has_next))
    def _():
        halo[half : 2 * half] = jnp.zeros((half, length), BF16)

    line_out = halo[...]
    count_t = length // LANES
    parts = []
    for b in range(count_t):
        now = line_out[:, b * LANES : (b + 1) * LANES]
        before = line_out[:, (b - 1) * LANES : b * LANES] if b else jnp.zeros_like(now)
        parts.append(jnp.concatenate([before, now], axis=1))
    y = dot(jnp.concatenate(parts, axis=0), block).astype(BF16)
    for b in range(count_t):
        at = (count_t - 1 - b) * LANES
        mine = y[b * 2 * half : (b + 1) * 2 * half]
        band[0:half, at : at + LANES] = mine[:half]
        band[half + rows : spread, at : at + LANES] = mine[half:]

    padded = band[...]

    def space(matrix):
        total = dot(matrix[:, 0:spread], padded)
        for i in (1, 2):
            total = total + dot(matrix[:, i * spread : (i + 1) * spread], padded)
        return total.astype(BF16)

    sources = space(source_mix)
    send[...] = sources
    copies = []
    for k in range(1, chans):
        copy = pltpu.make_async_remote_copy(
            src_ref=send, dst_ref=slots.at[ch],
            send_sem=send_sem.at[k], recv_sem=recv_sem.at[k],
            device_id=(sec, (ch + k) % chans), device_id_type=pl.DeviceIdType.MESH,
        )
        copy.start()
        copies.append(copy)
    slots[ch] = sources

    own = space(mix).astype(F32)
    keep = iota((MINOR, length), 1) >= iota((MINOR, length), 0)
    for c in range(0, rows, 2):
        pair = []
        for r in (c, c + 1):
            wide = jnp.broadcast_to(own[r : r + 1, :], (MINOR, length))
            wide = pltpu.roll(wide, 0, 1, stride=1, stride_axis=0)
            pair.append(jnp.where(keep, wide, 0.0))
        shifted_ref[c * MINOR : (c + 2) * MINOR, :] = jnp.concatenate(pair, axis=0).astype(BF16)

    for copy in copies:
        copy.wait()
    for j in range(chans):
        gathered_ref[j * SLOT : (j + 1) * SLOT, :] = slots[j]


def correlate_kernel(per, gathered_ref, shifted_ref, out_ref, weights, blocks, sems):
    slots, length = gathered_ref.shape
    rows, lags, total = out_ref.shape
    lanes = pl.cdiv(total, LANES) * LANES
    row, col = iota((lanes, slots), 0), iota((lanes, slots), 1)
    chosen = jnp.logical_and(col == row // per * SLOT + row % per, row < total)
    sources = dot(chosen.astype(F32).astype(BF16), gathered_ref[...])
    time = iota((lanes, length), 1)
    scale = 1.0 / length**0.5
    copies = []
    for k in range(lags // (2 * MINOR)):
        for h in range(2):
            shift = (2 * k + h) * MINOR
            moved = sources
            if shift:
                moved = jnp.where(time < length - shift, pltpu.roll(sources, length - shift, 1), 0.0)
            weights[k, h * lanes : (h + 1) * lanes, :] = moved.astype(BF16)
        result = dot(shifted_ref[...], weights[k], ((1,), (1,))) * scale
        low = result[:, 0:total].reshape(rows, MINOR, total)
        high = result[:, lanes : lanes + total].reshape(rows, MINOR, total)
        blocks[k] = jnp.concatenate([low, high], axis=1).astype(BF16)
        copy = pltpu.make_async_copy(
            blocks.at[k], out_ref.at[:, k * 2 * MINOR : (k + 1) * 2 * MINOR, :], sems.at[k]
        )
        copy.start()
        copies.append(copy)
    for copy in copies:
        copy.wait()


def shards(sections, chans, raw_traces, fir_taps, space_taps, source_index):
    rows, length = raw_traces.shape
    half = (space_taps.shape[0] - 1) // 2
    per = source_index.shape[1]
    total = per * chans
    lanes = -(-total // LANES) * LANES
    steps = LAGS // (2 * MINOR)
    vmem, smem = pl.BlockSpec(memory_space=pltpu.VMEM), pl.BlockSpec(memory_space=pltpu.SMEM)
    gathered, shifted = pl.pallas_call(
        functools.partial(exchange_kernel, sections, chans),
        out_shape=(
            jax.ShapeDtypeStruct((chans * SLOT, length), BF16),
            jax.ShapeDtypeStruct((rows * MINOR, length), BF16),
        ),
        in_specs=[smem, smem, vmem, vmem],
        out_specs=(vmem, vmem),
        scratch_shapes=[
            pltpu.VMEM((8, 2 * LANES), F32),
            pltpu.VMEM((rows + 2 * half, length), BF16),
            pltpu.VMEM((2 * half, length), BF16),
            pltpu.VMEM((SLOT, length), BF16),
            pltpu.VMEM((chans, SLOT, length), BF16),
            pltpu.SemaphoreType.DMA((2,)),
            pltpu.SemaphoreType.DMA((2,)),
            pltpu.SemaphoreType.DMA((chans,)),
            pltpu.SemaphoreType.DMA((chans,)),
        ],
        compiler_params=pltpu.CompilerParams(
            collective_id=0, has_side_effects=True, vmem_limit_bytes=24 * 2**20
        ),
        name="exchange",
    )(source_index, space_taps, fir_taps.reshape(1, -1), raw_traces)
    return pl.pallas_call(
        functools.partial(correlate_kernel, per),
        out_shape=jax.ShapeDtypeStruct((rows, LAGS, total), BF16),
        in_specs=[vmem, vmem],
        out_specs=pl.BlockSpec(memory_space=pl.ANY),
        scratch_shapes=[
            pltpu.VMEM((steps, 2 * lanes, length), BF16),
            pltpu.VMEM((steps, rows, 2 * MINOR, total), BF16),
            pltpu.SemaphoreType.DMA((steps,)),
        ],
        compiler_params=pltpu.CompilerParams(vmem_limit_bytes=40 * 2**20),
        name="correlate",
    )(gathered, shifted)


def solution(mesh):
    return jax.shard_map(
        functools.partial(shards, mesh.shape["section"], mesh.shape["chan"]),
        mesh=mesh,
        in_specs=(P(("section", "chan"), None), P(), P(), P("section", "chan")),
        out_specs=P(("section", "chan"), None, None),
        check_vma=False,
    )
```

```python
import functools

import jax
import jax.numpy as jnp
from jax import lax
from jax.experimental import pallas as pl
from jax.experimental.pallas import tpu as pltpu
from jax.sharding import PartitionSpec as P

LAGS = 64
MINOR = 8
SLOT = 8
LANES = 128
MESH = pl.DeviceIdType.MESH
F32, BF16 = jnp.float32, jnp.bfloat16


def iota(shape, dim):
    return lax.broadcasted_iota(jnp.int32, shape, dim)


def dot(a, b, contract=((1,), (0,))):
    return lax.dot_general(a, b, (contract, ((), ())), preferred_element_type=F32)


def fir_block(fir_ref, line_ref):
    taps = fir_ref.shape[1]
    line_ref[...] = jnp.zeros(line_ref.shape, F32)
    line_ref[0:1, 0:taps] = fir_ref[...].astype(F32)
    wide = jnp.broadcast_to(line_ref[0:1, 0 : 2 * LANES], (2 * LANES, 2 * LANES))
    toeplitz = pltpu.roll(wide, LANES, 1, stride=1, stride_axis=0)[:, :LANES]
    flip = (iota((LANES, LANES), 0) + iota((LANES, LANES), 1) == LANES - 1).astype(F32)
    return dot(toeplitz.astype(BF16), flip.astype(BF16)).astype(BF16)


def fir(x, block):
    rows, length = x.shape
    count = length // LANES
    parts = []
    for b in range(count):
        now = x[:, b * LANES : (b + 1) * LANES]
        before = x[:, (b - 1) * LANES : b * LANES] if b else jnp.zeros_like(now)
        parts.append(jnp.concatenate([before, now], axis=1))
    y = dot(jnp.concatenate(parts, axis=0), block).astype(BF16)
    return [y[b * rows : (b + 1) * rows] for b in reversed(range(count))]


def split3(x):
    high = x.astype(BF16)
    rest = x - high.astype(F32)
    middle = rest.astype(BF16)
    low = (rest - middle.astype(F32)).astype(BF16)
    return high, middle, low


def exchange_kernel(
    sections, chans,
    index_hbm, space_hbm, fir_hbm, raw_hbm,
    gathered_ref, shifted_ref,
    index_ref, space_ref, fir_ref, raw_ref, line, band, halo, own_ref,
    load_sem, halo_send, halo_recv, z_send, z_recv, x_send, x_recv,
):
    rows, length = raw_ref.shape
    half = halo.shape[0] // 2
    sec, ch = lax.axis_index("section"), lax.axis_index("chan")
    me = sec * chans + ch
    last = sections * chans - 1
    has_prev, has_next = me > 0, me < last
    prev = jnp.maximum(me - 1, 0)
    after = jnp.minimum(me + 1, last)
    prev_id = (prev // chans, prev % chans)
    next_id = (after // chans, after % chans)
    partner = ch + 1 - 2 * (ch % 2)

    barrier = pltpu.get_barrier_semaphore()
    for k in range(1, chans):
        pl.semaphore_signal(barrier, inc=1, device_id=(sec, (ch + k) % chans), device_id_type=MESH)
    cross_prev = jnp.logical_and(ch == 0, has_prev)
    cross_next = jnp.logical_and(ch == chans - 1, has_next)

    @pl.when(cross_prev)
    def _():
        pl.semaphore_signal(barrier, inc=1, device_id=prev_id, device_id_type=MESH)

    @pl.when(cross_next)
    def _():
        pl.semaphore_signal(barrier, inc=1, device_id=next_id, device_id_type=MESH)

    load_raw = pltpu.make_async_copy(raw_hbm, raw_ref, load_sem.at[0])
    load_fir = pltpu.make_async_copy(fir_hbm, fir_ref, load_sem.at[1])
    load_space = pltpu.make_async_copy(space_hbm, space_ref, load_sem.at[2])
    load_index = pltpu.make_async_copy(index_hbm, index_ref, load_sem.at[3])
    load_fir.start()
    load_raw.start()
    load_space.start()
    load_index.start()
    load_fir.wait()
    block = fir_block(fir_ref, line)

    pl.semaphore_wait(
        barrier, chans - 1 + cross_prev.astype(jnp.int32) + cross_next.astype(jnp.int32)
    )

    to_next = pltpu.make_async_remote_copy(
        src_ref=raw_hbm.at[rows - half : rows], dst_ref=halo.at[0:half],
        send_sem=halo_send.at[0], recv_sem=halo_recv.at[0],
        device_id=next_id, device_id_type=MESH,
    )
    to_prev = pltpu.make_async_remote_copy(
        src_ref=raw_hbm.at[0:half], dst_ref=halo.at[half : 2 * half],
        send_sem=halo_send.at[1], recv_sem=halo_recv.at[1],
        device_id=prev_id, device_id_type=MESH,
    )

    @pl.when(has_next)
    def _():
        to_next.start()

    @pl.when(has_prev)
    def _():
        to_prev.start()

    load_raw.wait()
    own = fir(raw_ref[...], block)
    for b, part in enumerate(own):
        band[half : half + rows, b * LANES : (b + 1) * LANES] = part

    load_space.wait()
    load_index.wait()
    taps = space_ref.shape[0]
    spread = rows + 2 * half
    offset = iota((rows, spread), 1) - iota((rows, spread), 0)
    mix = jnp.zeros((rows, spread), F32)
    for j in range(taps):
        mix = jnp.where(offset == j, space_ref[j], mix)
    mix = jnp.concatenate(split3(mix), axis=1)
    count = index_ref.shape[1]
    row, col = iota((2 * SLOT, rows), 0), iota((2 * SLOT, rows), 1)
    pick = jnp.zeros((2 * SLOT, rows), F32)
    for i in range(2 * SLOT):
        source = index_ref[0, i if i < count else i - (count - SLOT)] - ch * rows
        pick = jnp.where(jnp.logical_and(row == i, col == source), 1.0, pick)
    source_mix = dot(pick.astype(BF16), mix).astype(BF16)

    @pl.when(has_prev)
    def _():
        to_next.wait_recv()

    @pl.when(jnp.logical_not(has_prev))
    def _():
        halo[0:half] = jnp.zeros((half, length), BF16)

    @pl.when(has_next)
    def _():
        to_prev.wait_recv()

    @pl.when(jnp.logical_not(has_next))
    def _():
        halo[half : 2 * half] = jnp.zeros((half, length), BF16)

    for b, part in enumerate(fir(halo[...], block)):
        band[0:half, b * LANES : (b + 1) * LANES] = part[:half]
        band[half + rows : spread, b * LANES : (b + 1) * LANES] = part[half:]
    padded = band[...]

    def space(matrix):
        total = dot(matrix[:, 0:spread], padded)
        for i in (1, 2):
            total = total + dot(matrix[:, i * spread : (i + 1) * spread], padded)
        return total

    sources = space(source_mix)
    middle = length // 2
    tail = jnp.where(
        iota((SLOT, middle), 0) < SLOT // 2,
        sources[SLOT : 2 * SLOT, 0:middle], sources[SLOT : 2 * SLOT, middle:length],
    )
    gathered_ref[ch] = jnp.concatenate([sources[0:SLOT], tail], axis=1).astype(BF16)

    def piece(owner, target, send_sem, recv_sem):
        return pltpu.make_async_remote_copy(
            src_ref=gathered_ref.at[owner], dst_ref=gathered_ref.at[owner],
            send_sem=send_sem, recv_sem=recv_sem,
            device_id=(sec, target), device_id_type=MESH,
        )

    hops = chans // 2
    over_z = [
        piece(ch, (ch + 2 * k) % chans, z_send.at[k], z_recv.at[k]) for k in range(1, hops)
    ]
    for copy in over_z:
        copy.start()
    over_x = [piece(ch, partner, x_send.at[0], x_recv.at[0])]
    over_x[0].start()

    own_ref[...] = space(mix).astype(BF16).astype(F32)

    def shift(first, end):
        keep = iota((MINOR, length), 1) >= iota((MINOR, length), 0)
        for c in range(first, end, 2):
            pair = []
            for r in (c, c + 1):
                wide = jnp.broadcast_to(own_ref[r : r + 1, :], (MINOR, length))
                wide = pltpu.roll(wide, 0, 1, stride=1, stride_axis=0)
                pair.append(jnp.where(keep, wide, 0.0))
            joined = jnp.concatenate(pair, axis=0).astype(BF16)
            shifted_ref[c * MINOR : (c + 2) * MINOR, :] = joined

    shift(0, rows // 2)
    for k in range(1, hops):
        over_z[k - 1].wait_recv()
        owner = (ch + chans - 2 * k) % chans
        copy = piece(owner, partner, x_send.at[k], x_recv.at[k])
        copy.start()
        over_x.append(copy)
    shift(rows // 2, rows)

    @pl.when(has_next)
    def _():
        to_next.wait_send()

    @pl.when(has_prev)
    def _():
        to_prev.wait_send()

    for copy in over_z:
        copy.wait_send()
    for copy in over_x:
        copy.wait()


def correlate_kernel(per, gathered_ref, shifted_ref, out_ref, weights, blocks, sems):
    chans, _, packet = gathered_ref.shape
    length = shifted_ref.shape[1]
    middle = packet - length
    rows, lags, total = out_ref.shape
    lanes = pl.cdiv(total, LANES) * LANES
    packets = [gathered_ref[j].astype(F32) for j in range(chans)]
    packets = jnp.concatenate(packets, axis=0).astype(BF16)
    row, col = iota((lanes, chans * SLOT), 0), iota((lanes, chans * SLOT), 1)
    same = jnp.logical_and(col // SLOT == row // per, row < total)

    def choose(rank):
        chosen = jnp.logical_and(same, col % SLOT == rank)
        return chosen.astype(F32).astype(BF16)

    rank = row % per
    whole = choose(rank)
    halves = [
        choose(jnp.where(rank < SLOT, -1, rank - SLOT + h * (SLOT // 2))) for h in range(2)
    ]
    sources = jnp.concatenate(
        [
            dot(whole, packets[:, h * middle : (h + 1) * middle])
            + dot(halves[h], packets[:, length:packet])
            for h in range(2)
        ],
        axis=1,
    )
    time = iota((lanes, length), 1)
    scale = 1.0 / length**0.5
    copies = []
    for k in range(lags // (2 * MINOR)):
        for h in range(2):
            shift = (2 * k + h) * MINOR
            moved = sources
            if shift:
                moved = jnp.where(time < length - shift, pltpu.roll(sources, length - shift, 1), 0.0)
            weights[k, h * lanes : (h + 1) * lanes, :] = moved.astype(BF16)
        result = dot(shifted_ref[...], weights[k], ((1,), (1,))) * scale
        low = result[:, 0:total].reshape(rows, MINOR, total)
        high = result[:, lanes : lanes + total].reshape(rows, MINOR, total)
        blocks[k] = jnp.concatenate([low, high], axis=1).astype(BF16)
        copy = pltpu.make_async_copy(
            blocks.at[k], out_ref.at[:, k * 2 * MINOR : (k + 1) * 2 * MINOR, :], sems.at[k]
        )
        copy.start()
        copies.append(copy)
    for copy in copies:
        copy.wait()


def shards(sections, chans, raw_traces, fir_taps, space_taps, source_index):
    rows, length = raw_traces.shape
    half = (space_taps.shape[0] - 1) // 2
    per = source_index.shape[1]
    total = per * chans
    lanes = -(-total // LANES) * LANES
    steps = LAGS // (2 * MINOR)
    vmem, hbm = pl.BlockSpec(memory_space=pltpu.VMEM), pl.BlockSpec(memory_space=pltpu.HBM)
    hops = chans // 2
    gathered, shifted = pl.pallas_call(
        functools.partial(exchange_kernel, sections, chans),
        out_shape=(
            jax.ShapeDtypeStruct((chans, SLOT, length + length // 2), BF16),
            jax.ShapeDtypeStruct((rows * MINOR, length), BF16),
        ),
        in_specs=[hbm, hbm, hbm, hbm],
        out_specs=(vmem, vmem),
        scratch_shapes=[
            pltpu.SMEM(source_index.shape, jnp.int32),
            pltpu.SMEM(space_taps.shape, F32),
            pltpu.VMEM((1, fir_taps.shape[0]), BF16),
            pltpu.VMEM((rows, length), BF16),
            pltpu.VMEM((8, 2 * LANES), F32),
            pltpu.VMEM((rows + 2 * half, length), BF16),
            pltpu.VMEM((2 * half, length), BF16),
            pltpu.VMEM((rows, length), F32),
            pltpu.SemaphoreType.DMA((4,)),
            pltpu.SemaphoreType.DMA((2,)),
            pltpu.SemaphoreType.DMA((2,)),
            pltpu.SemaphoreType.DMA((hops,)),
            pltpu.SemaphoreType.DMA((hops,)),
            pltpu.SemaphoreType.DMA((hops,)),
            pltpu.SemaphoreType.DMA((hops,)),
        ],
        compiler_params=pltpu.CompilerParams(
            collective_id=0, has_side_effects=True, vmem_limit_bytes=24 * 2**20
        ),
        name="exchange",
    )(
        *(
            pltpu.with_memory_space_constraint(x, pltpu.HBM)
            for x in (source_index, space_taps, fir_taps.reshape(1, -1), raw_traces)
        )
    )
    return pl.pallas_call(
        functools.partial(correlate_kernel, per),
        out_shape=jax.ShapeDtypeStruct((rows, LAGS, total), BF16),
        in_specs=[vmem, vmem],
        out_specs=pl.BlockSpec(memory_space=pl.ANY),
        scratch_shapes=[
            pltpu.VMEM((steps, 2 * lanes, length), BF16),
            pltpu.VMEM((steps, rows, 2 * MINOR, total), BF16),
            pltpu.SemaphoreType.DMA((steps,)),
        ],
        compiler_params=pltpu.CompilerParams(vmem_limit_bytes=40 * 2**20),
        name="correlate",
    )(gathered, shifted)


def solution(mesh):
    return jax.shard_map(
        functools.partial(shards, mesh.shape["section"], mesh.shape["chan"]),
        mesh=mesh,
        in_specs=(P(("section", "chan"), None), P(), P(), P("section", "chan")),
        out_specs=P(("section", "chan"), None, None),
        check_vma=False,
    )
```

```python
import functools

import jax
import jax.numpy as jnp
from jax import lax
from jax.experimental import pallas as pl
from jax.experimental.pallas import tpu as pltpu
from jax.sharding import PartitionSpec as P

LAGS = 64
MINOR = 8
SLOT = 8
LANES = 128
MESH = pl.DeviceIdType.MESH
F32, BF16 = jnp.float32, jnp.bfloat16


def iota(shape, dim):
    return lax.broadcasted_iota(jnp.int32, shape, dim)


def dot(a, b, contract=((1,), (0,))):
    return lax.dot_general(a, b, (contract, ((), ())), preferred_element_type=F32)


def fir_block(fir_ref, line_ref):
    taps = fir_ref.shape[1]
    line_ref[...] = jnp.zeros(line_ref.shape, F32)
    line_ref[0:1, 0:taps] = fir_ref[...].astype(F32)
    wide = jnp.broadcast_to(line_ref[0:1, 0 : 2 * LANES], (2 * LANES, 2 * LANES))
    toeplitz = pltpu.roll(wide, LANES, 1, stride=1, stride_axis=0)[:, :LANES]
    flip = (iota((LANES, LANES), 0) + iota((LANES, LANES), 1) == LANES - 1).astype(F32)
    return dot(toeplitz.astype(BF16), flip.astype(BF16)).astype(BF16)


def fir(x, block):
    rows, length = x.shape
    count = length // LANES
    parts = []
    for b in range(count):
        now = x[:, b * LANES : (b + 1) * LANES]
        before = x[:, (b - 1) * LANES : b * LANES] if b else jnp.zeros_like(now)
        parts.append(jnp.concatenate([before, now], axis=1))
    y = dot(jnp.concatenate(parts, axis=0), block).astype(BF16)
    return [y[b * rows : (b + 1) * rows] for b in reversed(range(count))]


def split3(x):
    high = x.astype(BF16)
    rest = x - high.astype(F32)
    middle = rest.astype(BF16)
    low = (rest - middle.astype(F32)).astype(BF16)
    return high, middle, low


def exchange_kernel(
    sections, chans,
    index_hbm, space_hbm, fir_hbm, raw_hbm,
    gathered_ref, shifted_ref,
    index_ref, space_ref, fir_ref, raw_ref, line, band, halo, own_ref, source_ref,
    load_sem, halo_send, halo_recv, send_sem, recv_sem,
):
    rows, length = raw_ref.shape
    half = halo.shape[0] // 2
    sec, ch = lax.axis_index("section"), lax.axis_index("chan")
    me = sec * chans + ch
    last = sections * chans - 1
    has_prev, has_next = me > 0, me < last
    prev = jnp.maximum(me - 1, 0)
    after = jnp.minimum(me + 1, last)
    prev_id = (prev // chans, prev % chans)
    next_id = (after // chans, after % chans)

    load_raw = pltpu.make_async_copy(raw_hbm, raw_ref, load_sem.at[0])
    load_fir = pltpu.make_async_copy(fir_hbm, fir_ref, load_sem.at[1])
    load_space = pltpu.make_async_copy(space_hbm, space_ref, load_sem.at[2])
    load_index = pltpu.make_async_copy(index_hbm, index_ref, load_sem.at[3])
    load_fir.start()
    load_raw.start()
    load_space.start()
    load_index.start()

    barrier = pltpu.get_barrier_semaphore()
    cross_prev = jnp.logical_and(ch == 0, has_prev)
    cross_next = jnp.logical_and(ch == chans - 1, has_next)

    @pl.when(cross_prev)
    def _():
        pl.semaphore_signal(barrier, inc=1, device_id=prev_id, device_id_type=MESH)

    @pl.when(cross_next)
    def _():
        pl.semaphore_signal(barrier, inc=1, device_id=next_id, device_id_type=MESH)

    for k in range(1, chans):
        pl.semaphore_signal(barrier, inc=1, device_id=(sec, (ch + k) % chans), device_id_type=MESH)

    load_space.wait()
    load_index.wait()
    taps = space_ref.shape[0]

    def mixing(width, place):
        offset = place(iota((rows, width), 1)) - iota((rows, width), 0)
        mix = jnp.zeros((rows, width), F32)
        for j in range(taps):
            mix = jnp.where(offset == j, space_ref[j], mix)
        return jnp.concatenate(split3(mix), axis=1)

    mix_own = mixing(rows, lambda col: col + half)
    mix_halo = mixing(2 * half, lambda col: jnp.where(col < half, col, col + rows))
    count = index_ref.shape[1]
    row, col = iota((2 * SLOT, rows), 0), iota((2 * SLOT, rows), 1)
    pick = jnp.zeros((2 * SLOT, rows), F32)
    for i in range(2 * SLOT):
        source = index_ref[0, i if i < count else i - (count - SLOT)] - ch * rows
        pick = jnp.where(jnp.logical_and(row == i, col == source), 1.0, pick)
    pick = pick.astype(BF16)
    source_own = dot(pick, mix_own).astype(BF16)
    source_halo = dot(pick, mix_halo).astype(BF16)

    load_fir.wait()
    block = fir_block(fir_ref, line)
    load_raw.wait()
    for b, part in enumerate(fir(raw_ref[...], block)):
        band[:, b * LANES : (b + 1) * LANES] = part
    thrice = jnp.concatenate([band[...]] * 3, axis=0)
    own_ref[...] = dot(mix_own, thrice)
    source_ref[...] = dot(source_own, thrice)

    pl.semaphore_wait(
        barrier, chans - 1 + cross_prev.astype(jnp.int32) + cross_next.astype(jnp.int32)
    )

    to_next = pltpu.make_async_remote_copy(
        src_ref=band.at[rows - half : rows], dst_ref=halo.at[0:half],
        send_sem=halo_send.at[0], recv_sem=halo_recv.at[0],
        device_id=next_id, device_id_type=MESH,
    )
    to_prev = pltpu.make_async_remote_copy(
        src_ref=band.at[0:half], dst_ref=halo.at[half : 2 * half],
        send_sem=halo_send.at[1], recv_sem=halo_recv.at[1],
        device_id=prev_id, device_id_type=MESH,
    )

    @pl.when(has_next)
    def _():
        to_next.start()

    @pl.when(has_prev)
    def _():
        to_prev.start()

    @pl.when(has_prev)
    def _():
        to_next.wait_recv()

    @pl.when(jnp.logical_not(has_prev))
    def _():
        halo[0:half] = jnp.zeros((half, length), BF16)

    @pl.when(has_next)
    def _():
        to_prev.wait_recv()

    @pl.when(jnp.logical_not(has_next))
    def _():
        halo[half : 2 * half] = jnp.zeros((half, length), BF16)

    edges = jnp.concatenate([halo[...]] * 3, axis=0)
    sources = source_ref[...] + dot(source_halo, edges)
    middle = length // 2
    tail = jnp.where(
        iota((SLOT, middle), 0) < SLOT // 2,
        sources[SLOT : 2 * SLOT, 0:middle], sources[SLOT : 2 * SLOT, middle:length],
    )
    gathered_ref[ch] = jnp.concatenate([sources[0:SLOT], tail], axis=1).astype(BF16)

    copies = []
    for k in sorted(range(1, chans), key=lambda k: abs(2 * k - chans)):
        copy = pltpu.make_async_remote_copy(
            src_ref=gathered_ref.at[ch], dst_ref=gathered_ref.at[ch],
            send_sem=send_sem.at[k], recv_sem=recv_sem.at[k],
            device_id=(sec, (ch + k) % chans), device_id_type=MESH,
        )
        copy.start()
        copies.append(copy)

    own_ref[...] = (own_ref[...] + dot(mix_halo, edges)).astype(BF16).astype(F32)
    keep = iota((MINOR, length), 1) >= iota((MINOR, length), 0)
    for c in range(0, rows, 2):
        pair = []
        for r in (c, c + 1):
            wide = jnp.broadcast_to(own_ref[r : r + 1, :], (MINOR, length))
            wide = pltpu.roll(wide, 0, 1, stride=1, stride_axis=0)
            pair.append(jnp.where(keep, wide, 0.0))
        shifted_ref[c * MINOR : (c + 2) * MINOR, :] = jnp.concatenate(pair, axis=0).astype(BF16)

    @pl.when(has_next)
    def _():
        to_next.wait_send()

    @pl.when(has_prev)
    def _():
        to_prev.wait_send()

    for copy in copies:
        copy.wait()


def correlate_kernel(per, gathered_ref, shifted_ref, out_ref, weights, blocks, sems):
    chans, _, packet = gathered_ref.shape
    length = shifted_ref.shape[1]
    middle = packet - length
    rows, lags, total = out_ref.shape
    lanes = pl.cdiv(total, LANES) * LANES
    packets = [gathered_ref[j].astype(F32) for j in range(chans)]
    packets = jnp.concatenate(packets, axis=0).astype(BF16)
    row, col = iota((lanes, chans * SLOT), 0), iota((lanes, chans * SLOT), 1)
    same = jnp.logical_and(col // SLOT == row // per, row < total)

    def choose(rank):
        chosen = jnp.logical_and(same, col % SLOT == rank)
        return chosen.astype(F32).astype(BF16)

    rank = row % per
    whole = choose(rank)
    halves = [
        choose(jnp.where(rank < SLOT, -1, rank - SLOT + h * (SLOT // 2))) for h in range(2)
    ]
    sources = jnp.concatenate(
        [
            dot(whole, packets[:, h * middle : (h + 1) * middle])
            + dot(halves[h], packets[:, length:packet])
            for h in range(2)
        ],
        axis=1,
    )
    time = iota((lanes, length), 1)
    scale = 1.0 / length**0.5
    copies = []
    for k in range(lags // (2 * MINOR)):
        for h in range(2):
            shift = (2 * k + h) * MINOR
            moved = sources
            if shift:
                moved = jnp.where(time < length - shift, pltpu.roll(sources, length - shift, 1), 0.0)
            weights[k, h * lanes : (h + 1) * lanes, :] = moved.astype(BF16)
        result = dot(shifted_ref[...], weights[k], ((1,), (1,))) * scale
        low = result[:, 0:total].reshape(rows, MINOR, total)
        high = result[:, lanes : lanes + total].reshape(rows, MINOR, total)
        blocks[k] = jnp.concatenate([low, high], axis=1).astype(BF16)
        copy = pltpu.make_async_copy(
            blocks.at[k], out_ref.at[:, k * 2 * MINOR : (k + 1) * 2 * MINOR, :], sems.at[k]
        )
        copy.start()
        copies.append(copy)
    for copy in copies:
        copy.wait()


def shards(sections, chans, raw_traces, fir_taps, space_taps, source_index):
    rows, length = raw_traces.shape
    half = (space_taps.shape[0] - 1) // 2
    per = source_index.shape[1]
    total = per * chans
    lanes = -(-total // LANES) * LANES
    steps = LAGS // (2 * MINOR)
    vmem, hbm = pl.BlockSpec(memory_space=pltpu.VMEM), pl.BlockSpec(memory_space=pltpu.HBM)
    gathered, shifted = pl.pallas_call(
        functools.partial(exchange_kernel, sections, chans),
        out_shape=(
            jax.ShapeDtypeStruct((chans, SLOT, length + length // 2), BF16),
            jax.ShapeDtypeStruct((rows * MINOR, length), BF16),
        ),
        in_specs=[hbm, hbm, hbm, hbm],
        out_specs=(vmem, vmem),
        scratch_shapes=[
            pltpu.SMEM(source_index.shape, jnp.int32),
            pltpu.SMEM(space_taps.shape, F32),
            pltpu.VMEM((1, fir_taps.shape[0]), BF16),
            pltpu.VMEM((rows, length), BF16),
            pltpu.VMEM((8, 2 * LANES), F32),
            pltpu.VMEM((rows, length), BF16),
            pltpu.VMEM((2 * half, length), BF16),
            pltpu.VMEM((rows, length), F32),
            pltpu.VMEM((2 * SLOT, length), F32),
            pltpu.SemaphoreType.DMA((4,)),
            pltpu.SemaphoreType.DMA((2,)),
            pltpu.SemaphoreType.DMA((2,)),
            pltpu.SemaphoreType.DMA((chans,)),
            pltpu.SemaphoreType.DMA((chans,)),
        ],
        compiler_params=pltpu.CompilerParams(
            collective_id=0, has_side_effects=True, vmem_limit_bytes=24 * 2**20
        ),
        name="exchange",
    )(
        *(
            pltpu.with_memory_space_constraint(x, pltpu.HBM)
            for x in (source_index, space_taps, fir_taps.reshape(1, -1), raw_traces)
        )
    )
    return pl.pallas_call(
        functools.partial(correlate_kernel, per),
        out_shape=jax.ShapeDtypeStruct((rows, LAGS, total), BF16),
        in_specs=[vmem, vmem],
        out_specs=pl.BlockSpec(memory_space=pl.ANY),
        scratch_shapes=[
            pltpu.VMEM((steps, 2 * lanes, length), BF16),
            pltpu.VMEM((steps, rows, 2 * MINOR, total), BF16),
            pltpu.SemaphoreType.DMA((steps,)),
        ],
        compiler_params=pltpu.CompilerParams(vmem_limit_bytes=40 * 2**20),
        name="correlate",
    )(gathered, shifted)


def solution(mesh):
    return jax.shard_map(
        functools.partial(shards, mesh.shape["section"], mesh.shape["chan"]),
        mesh=mesh,
        in_specs=(P(("section", "chan"), None), P(), P(), P("section", "chan")),
        out_specs=P(("section", "chan"), None, None),
        check_vma=False,
    )
```

```python
import functools

import jax
import jax.numpy as jnp
from jax import lax
from jax.experimental import pallas as pl
from jax.experimental.pallas import tpu as pltpu
from jax.sharding import PartitionSpec as P

LAGS = 64
MINOR = 8
SLOT = 8
LANES = 128
MESH = pl.DeviceIdType.MESH
F32, BF16 = jnp.float32, jnp.bfloat16


def iota(shape, dim):
    return lax.broadcasted_iota(jnp.int32, shape, dim)


def dot(a, b, contract=((1,), (0,))):
    return lax.dot_general(a, b, (contract, ((), ())), preferred_element_type=F32)


def fir_block(fir_ref, line_ref):
    taps = fir_ref.shape[1]
    line_ref[...] = jnp.zeros(line_ref.shape, F32)
    line_ref[0:1, 0:taps] = fir_ref[...].astype(F32)
    wide = jnp.broadcast_to(line_ref[0:1, 0 : 2 * LANES], (2 * LANES, 2 * LANES))
    toeplitz = pltpu.roll(wide, LANES, 1, stride=1, stride_axis=0)[:, :LANES]
    flip = (iota((LANES, LANES), 0) + iota((LANES, LANES), 1) == LANES - 1).astype(F32)
    return dot(toeplitz.astype(BF16), flip.astype(BF16)).astype(BF16)


def fir(x, block):
    rows, length = x.shape
    count = length // LANES
    parts = []
    for b in range(count):
        now = x[:, b * LANES : (b + 1) * LANES]
        before = x[:, (b - 1) * LANES : b * LANES] if b else jnp.zeros_like(now)
        parts.append(jnp.concatenate([before, now], axis=1))
    y = dot(jnp.concatenate(parts, axis=0), block).astype(BF16)
    return [y[b * rows : (b + 1) * rows] for b in reversed(range(count))]


def split3(x):
    high = x.astype(BF16)
    rest = x - high.astype(F32)
    middle = rest.astype(BF16)
    low = (rest - middle.astype(F32)).astype(BF16)
    return high, middle, low


def exchange_kernel(
    sections, chans,
    index_hbm, space_hbm, fir_hbm, raw_hbm,
    gathered_ref, shifted_ref,
    index_ref, space_ref, fir_ref, raw_ref, line, band, halo, own_ref, source_ref,
    load_sem, halo_send, halo_recv, send_sem, recv_sem,
):
    rows, length = raw_ref.shape
    half = halo.shape[0] // 2
    sec, ch = lax.axis_index("section"), lax.axis_index("chan")
    me = sec * chans + ch
    last = sections * chans - 1
    has_prev, has_next = me > 0, me < last
    prev = jnp.maximum(me - 1, 0)
    after = jnp.minimum(me + 1, last)
    prev_id = (prev // chans, prev % chans)
    next_id = (after // chans, after % chans)

    load_raw = pltpu.make_async_copy(raw_hbm, raw_ref, load_sem.at[0])
    load_fir = pltpu.make_async_copy(fir_hbm, fir_ref, load_sem.at[1])
    load_space = pltpu.make_async_copy(space_hbm, space_ref, load_sem.at[2])
    load_index = pltpu.make_async_copy(index_hbm, index_ref, load_sem.at[3])
    load_fir.start()
    load_raw.start()
    load_space.start()
    load_index.start()

    barrier = pltpu.get_barrier_semaphore()
    cross_prev = jnp.logical_and(ch == 0, has_prev)
    cross_next = jnp.logical_and(ch == chans - 1, has_next)

    @pl.when(cross_prev)
    def _():
        pl.semaphore_signal(barrier, inc=1, device_id=prev_id, device_id_type=MESH)

    @pl.when(cross_next)
    def _():
        pl.semaphore_signal(barrier, inc=1, device_id=next_id, device_id_type=MESH)

    for k in range(1, chans):
        pl.semaphore_signal(barrier, inc=1, device_id=(sec, (ch + k) % chans), device_id_type=MESH)

    load_space.wait()
    load_index.wait()
    taps = space_ref.shape[0]

    def mixing(width, place):
        offset = place(iota((rows, width), 1)) - iota((rows, width), 0)
        mix = jnp.zeros((rows, width), F32)
        for j in range(taps):
            mix = jnp.where(offset == j, space_ref[j], mix)
        return jnp.concatenate(split3(mix), axis=1)

    mix_own = mixing(rows, lambda col: col + half)
    mix_halo = mixing(2 * half, lambda col: jnp.where(col < half, col, col + rows))
    count = index_ref.shape[1]
    row, col = iota((2 * SLOT, rows), 0), iota((2 * SLOT, rows), 1)
    pick = jnp.zeros((2 * SLOT, rows), F32)
    for i in range(2 * SLOT):
        source = index_ref[0, i if i < count else i - (count - SLOT)] - ch * rows
        pick = jnp.where(jnp.logical_and(row == i, col == source), 1.0, pick)
    pick = pick.astype(BF16)
    source_own = dot(pick, mix_own).astype(BF16)
    source_halo = dot(pick, mix_halo).astype(BF16)

    load_fir.wait()
    block = fir_block(fir_ref, line)
    load_raw.wait()
    for b, part in enumerate(fir(raw_ref[...], block)):
        band[:, b * LANES : (b + 1) * LANES] = part
    thrice = jnp.concatenate([band[...]] * 3, axis=0)
    own_ref[...] = dot(mix_own, thrice)
    source_ref[...] = dot(source_own, thrice)

    pl.semaphore_wait(
        barrier, chans - 1 + cross_prev.astype(jnp.int32) + cross_next.astype(jnp.int32)
    )

    to_next = pltpu.make_async_remote_copy(
        src_ref=band.at[rows - half : rows], dst_ref=halo.at[0:half],
        send_sem=halo_send.at[0], recv_sem=halo_recv.at[0],
        device_id=next_id, device_id_type=MESH,
    )
    to_prev = pltpu.make_async_remote_copy(
        src_ref=band.at[0:half], dst_ref=halo.at[half : 2 * half],
        send_sem=halo_send.at[1], recv_sem=halo_recv.at[1],
        device_id=prev_id, device_id_type=MESH,
    )

    @pl.when(has_next)
    def _():
        to_next.start()

    @pl.when(has_prev)
    def _():
        to_prev.start()

    @pl.when(has_prev)
    def _():
        to_next.wait_recv()

    @pl.when(jnp.logical_not(has_prev))
    def _():
        halo[0:half] = jnp.zeros((half, length), BF16)

    @pl.when(has_next)
    def _():
        to_prev.wait_recv()

    @pl.when(jnp.logical_not(has_next))
    def _():
        halo[half : 2 * half] = jnp.zeros((half, length), BF16)

    edges = jnp.concatenate([halo[...]] * 3, axis=0)
    sources = source_ref[...] + dot(source_halo, edges)
    middle = length // 2
    tail = jnp.where(
        iota((SLOT, middle), 0) < SLOT // 2,
        sources[SLOT : 2 * SLOT, 0:middle], sources[SLOT : 2 * SLOT, middle:length],
    )
    gathered_ref[ch] = jnp.concatenate([sources[0:SLOT], tail], axis=1).astype(BF16)

    copies = []
    for k in range(1, chans):
        copy = pltpu.make_async_remote_copy(
            src_ref=gathered_ref.at[ch], dst_ref=gathered_ref.at[ch],
            send_sem=send_sem.at[k], recv_sem=recv_sem.at[k],
            device_id=(sec, (ch + k) % chans), device_id_type=MESH,
        )
        copy.start()
        copies.append(copy)

    own_ref[...] = (own_ref[...] + dot(mix_halo, edges)).astype(BF16).astype(F32)
    keep = iota((MINOR, length), 1) >= iota((MINOR, length), 0)
    for c in range(0, rows, 2):
        pair = []
        for r in (c, c + 1):
            wide = jnp.broadcast_to(own_ref[r : r + 1, :], (MINOR, length))
            wide = pltpu.roll(wide, 0, 1, stride=1, stride_axis=0)
            pair.append(jnp.where(keep, wide, 0.0))
        shifted_ref[c * MINOR : (c + 2) * MINOR, :] = jnp.concatenate(pair, axis=0).astype(BF16)

    @pl.when(has_next)
    def _():
        to_next.wait_send()

    @pl.when(has_prev)
    def _():
        to_prev.wait_send()

    for copy in copies:
        copy.wait()


def correlate_kernel(per, gathered_ref, shifted_ref, out_ref, weights, blocks, sems):
    chans, _, packet = gathered_ref.shape
    length = shifted_ref.shape[1]
    middle = packet - length
    rows, lags, total = out_ref.shape
    lanes = pl.cdiv(total, LANES) * LANES
    packets = [gathered_ref[j].astype(F32) for j in range(chans)]
    packets = jnp.concatenate(packets, axis=0).astype(BF16)
    row, col = iota((lanes, chans * SLOT), 0), iota((lanes, chans * SLOT), 1)
    same = jnp.logical_and(col // SLOT == row // per, row < total)

    def choose(rank):
        chosen = jnp.logical_and(same, col % SLOT == rank)
        return chosen.astype(F32).astype(BF16)

    rank = row % per
    whole = choose(rank)
    halves = [
        choose(jnp.where(rank < SLOT, -1, rank - SLOT + h * (SLOT // 2))) for h in range(2)
    ]
    sources = jnp.concatenate(
        [
            dot(whole, packets[:, h * middle : (h + 1) * middle])
            + dot(halves[h], packets[:, length:packet])
            for h in range(2)
        ],
        axis=1,
    )
    time = iota((lanes, length), 1)
    scale = 1.0 / length**0.5
    copies = []
    for k in range(lags // (2 * MINOR)):
        for h in range(2):
            shift = (2 * k + h) * MINOR
            moved = sources
            if shift:
                moved = jnp.where(time < length - shift, pltpu.roll(sources, length - shift, 1), 0.0)
            weights[k, h * lanes : (h + 1) * lanes, :] = moved.astype(BF16)
        result = dot(shifted_ref[...], weights[k], ((1,), (1,))) * scale
        low = result[:, 0:total].reshape(rows, MINOR, total)
        high = result[:, lanes : lanes + total].reshape(rows, MINOR, total)
        blocks[k] = jnp.concatenate([low, high], axis=1).astype(BF16)
        copy = pltpu.make_async_copy(
            blocks.at[k], out_ref.at[:, k * 2 * MINOR : (k + 1) * 2 * MINOR, :], sems.at[k]
        )
        copy.start()
        copies.append(copy)
    for copy in copies:
        copy.wait()


def shards(sections, chans, raw_traces, fir_taps, space_taps, source_index):
    rows, length = raw_traces.shape
    half = (space_taps.shape[0] - 1) // 2
    per = source_index.shape[1]
    total = per * chans
    lanes = -(-total // LANES) * LANES
    steps = LAGS // (2 * MINOR)
    vmem, hbm = pl.BlockSpec(memory_space=pltpu.VMEM), pl.BlockSpec(memory_space=pltpu.HBM)
    gathered, shifted = pl.pallas_call(
        functools.partial(exchange_kernel, sections, chans),
        out_shape=(
            jax.ShapeDtypeStruct((chans, SLOT, length + length // 2), BF16),
            jax.ShapeDtypeStruct((rows * MINOR, length), BF16),
        ),
        in_specs=[hbm, hbm, hbm, hbm],
        out_specs=(vmem, vmem),
        scratch_shapes=[
            pltpu.SMEM(source_index.shape, jnp.int32),
            pltpu.SMEM(space_taps.shape, F32),
            pltpu.VMEM((1, fir_taps.shape[0]), BF16),
            pltpu.VMEM((rows, length), BF16),
            pltpu.VMEM((8, 2 * LANES), F32),
            pltpu.VMEM((rows, length), BF16),
            pltpu.VMEM((2 * half, length), BF16),
            pltpu.VMEM((rows, length), F32),
            pltpu.VMEM((2 * SLOT, length), F32),
            pltpu.SemaphoreType.DMA((4,)),
            pltpu.SemaphoreType.DMA((2,)),
            pltpu.SemaphoreType.DMA((2,)),
            pltpu.SemaphoreType.DMA((chans,)),
            pltpu.SemaphoreType.DMA((chans,)),
        ],
        compiler_params=pltpu.CompilerParams(
            collective_id=0, has_side_effects=True, vmem_limit_bytes=24 * 2**20
        ),
        name="exchange",
    )(
        *(
            pltpu.with_memory_space_constraint(x, pltpu.HBM)
            for x in (source_index, space_taps, fir_taps.reshape(1, -1), raw_traces)
        )
    )
    return pl.pallas_call(
        functools.partial(correlate_kernel, per),
        out_shape=jax.ShapeDtypeStruct((rows, LAGS, total), BF16),
        in_specs=[vmem, vmem],
        out_specs=pl.BlockSpec(memory_space=pl.ANY),
        scratch_shapes=[
            pltpu.VMEM((steps, 2 * lanes, length), BF16),
            pltpu.VMEM((steps, rows, 2 * MINOR, total), BF16),
            pltpu.SemaphoreType.DMA((steps,)),
        ],
        compiler_params=pltpu.CompilerParams(vmem_limit_bytes=40 * 2**20),
        name="correlate",
    )(gathered, shifted)


def solution(mesh):
    return jax.shard_map(
        functools.partial(shards, mesh.shape["section"], mesh.shape["chan"]),
        mesh=mesh,
        in_specs=(P(("section", "chan"), None), P(), P(), P("section", "chan")),
        out_specs=P(("section", "chan"), None, None),
        check_vma=False,
    )
```

```python
import functools

import jax
import jax.numpy as jnp
from jax import lax
from jax.experimental import pallas as pl
from jax.experimental.pallas import tpu as pltpu
from jax.sharding import PartitionSpec as P

LAGS = 64
MINOR = 8
SLOT = 8
LANES = 128
MESH = pl.DeviceIdType.MESH
F32, BF16 = jnp.float32, jnp.bfloat16


def iota(shape, dim):
    return lax.broadcasted_iota(jnp.int32, shape, dim)


def dot(a, b, contract=((1,), (0,))):
    return lax.dot_general(a, b, (contract, ((), ())), preferred_element_type=F32)


def fir_block(fir_ref, line_ref):
    taps = fir_ref.shape[1]
    line_ref[...] = jnp.zeros(line_ref.shape, F32)
    line_ref[0:1, 0:taps] = fir_ref[...].astype(F32)
    wide = jnp.broadcast_to(line_ref[0:1, 0 : 2 * LANES], (2 * LANES, 2 * LANES))
    toeplitz = pltpu.roll(wide, LANES, 1, stride=1, stride_axis=0)[:, :LANES]
    flip = (iota((LANES, LANES), 0) + iota((LANES, LANES), 1) == LANES - 1).astype(F32)
    return dot(toeplitz.astype(BF16), flip.astype(BF16)).astype(BF16)


def fir(x, block):
    rows, length = x.shape
    count = length // LANES
    parts = []
    for b in range(count):
        now = x[:, b * LANES : (b + 1) * LANES]
        before = x[:, (b - 1) * LANES : b * LANES] if b else jnp.zeros_like(now)
        parts.append(jnp.concatenate([before, now], axis=1))
    y = dot(jnp.concatenate(parts, axis=0), block).astype(BF16)
    return [y[b * rows : (b + 1) * rows] for b in reversed(range(count))]


def split3(x):
    high = x.astype(BF16)
    rest = x - high.astype(F32)
    middle = rest.astype(BF16)
    low = (rest - middle.astype(F32)).astype(BF16)
    return high, middle, low


def exchange_kernel(
    sections, chans,
    index_hbm, space_hbm, fir_hbm, raw_hbm,
    gathered_ref, shifted_ref,
    index_ref, space_ref, fir_ref, raw_ref, line, band, halo, own_ref, source_ref,
    load_sem, halo_send, halo_recv, send_sem, recv_sem,
):
    rows, length = raw_ref.shape
    half = halo.shape[0] // 2
    sec, ch = lax.axis_index("section"), lax.axis_index("chan")
    me = sec * chans + ch
    last = sections * chans - 1
    has_prev, has_next = me > 0, me < last
    prev = jnp.maximum(me - 1, 0)
    after = jnp.minimum(me + 1, last)
    prev_id = (prev // chans, prev % chans)
    next_id = (after // chans, after % chans)

    load_raw = pltpu.make_async_copy(raw_hbm, raw_ref, load_sem.at[0])
    load_fir = pltpu.make_async_copy(fir_hbm, fir_ref, load_sem.at[1])
    load_space = pltpu.make_async_copy(space_hbm, space_ref, load_sem.at[2])
    load_index = pltpu.make_async_copy(index_hbm, index_ref, load_sem.at[3])
    load_fir.start()
    load_raw.start()
    load_space.start()
    load_index.start()

    barrier = pltpu.get_barrier_semaphore()
    cross_prev = jnp.logical_and(ch == 0, has_prev)
    cross_next = jnp.logical_and(ch == chans - 1, has_next)

    @pl.when(cross_prev)
    def _():
        pl.semaphore_signal(barrier, inc=1, device_id=prev_id, device_id_type=MESH)

    @pl.when(cross_next)
    def _():
        pl.semaphore_signal(barrier, inc=1, device_id=next_id, device_id_type=MESH)

    for k in range(1, chans):
        pl.semaphore_signal(barrier, inc=1, device_id=(sec, (ch + k) % chans), device_id_type=MESH)

    load_space.wait()
    load_index.wait()
    taps = space_ref.shape[0]

    def mixing(width, place):
        offset = place(iota((rows, width), 1)) - iota((rows, width), 0)
        mix = jnp.zeros((rows, width), F32)
        for j in range(taps):
            mix = jnp.where(offset == j, space_ref[j], mix)
        return jnp.concatenate(split3(mix), axis=1)

    mix_own = mixing(rows, lambda col: col + half)
    mix_halo = mixing(2 * half, lambda col: jnp.where(col < half, col, col + rows))
    count = index_ref.shape[1]
    row, col = iota((2 * SLOT, rows), 0), iota((2 * SLOT, rows), 1)
    pick = jnp.zeros((2 * SLOT, rows), F32)
    for i in range(2 * SLOT):
        source = index_ref[0, i if i < count else i - (count - SLOT)] - ch * rows
        pick = jnp.where(jnp.logical_and(row == i, col == source), 1.0, pick)
    pick = pick.astype(BF16)
    source_own = dot(pick, mix_own).astype(BF16)
    source_halo = dot(pick, mix_halo).astype(BF16)

    load_fir.wait()
    block = fir_block(fir_ref, line)
    load_raw.wait()
    for b, part in enumerate(fir(raw_ref[...], block)):
        band[:, b * LANES : (b + 1) * LANES] = part
    thrice = jnp.concatenate([band[...]] * 3, axis=0)
    own_ref[...] = dot(mix_own, thrice)
    source_ref[...] = dot(source_own, thrice)

    pl.semaphore_wait(
        barrier, chans - 1 + cross_prev.astype(jnp.int32) + cross_next.astype(jnp.int32)
    )

    to_next = pltpu.make_async_remote_copy(
        src_ref=band.at[rows - half : rows], dst_ref=halo.at[0:half],
        send_sem=halo_send.at[0], recv_sem=halo_recv.at[0],
        device_id=next_id, device_id_type=MESH,
    )
    to_prev = pltpu.make_async_remote_copy(
        src_ref=band.at[0:half], dst_ref=halo.at[half : 2 * half],
        send_sem=halo_send.at[1], recv_sem=halo_recv.at[1],
        device_id=prev_id, device_id_type=MESH,
    )

    @pl.when(has_next)
    def _():
        to_next.start()

    @pl.when(has_prev)
    def _():
        to_prev.start()

    @pl.when(has_prev)
    def _():
        to_next.wait_recv()

    @pl.when(jnp.logical_not(has_prev))
    def _():
        halo[0:half] = jnp.zeros((half, length), BF16)

    @pl.when(has_next)
    def _():
        to_prev.wait_recv()

    @pl.when(jnp.logical_not(has_next))
    def _():
        halo[half : 2 * half] = jnp.zeros((half, length), BF16)

    edges = jnp.concatenate([halo[...]] * 3, axis=0)
    sources = source_ref[...] + dot(source_halo, edges)
    middle = length // 2
    tail = jnp.where(
        iota((SLOT, middle), 0) < SLOT // 2,
        sources[SLOT : 2 * SLOT, 0:middle], sources[SLOT : 2 * SLOT, middle:length],
    )
    gathered_ref[ch] = jnp.concatenate([sources[0:SLOT], tail], axis=1).astype(BF16)

    copies = []
    for k in range(1, chans):
        copy = pltpu.make_async_remote_copy(
            src_ref=gathered_ref.at[ch], dst_ref=gathered_ref.at[ch],
            send_sem=send_sem.at[k], recv_sem=recv_sem.at[k],
            device_id=(sec, (ch + k) % chans), device_id_type=MESH,
        )
        copy.start()
        copies.append(copy)

    own_ref[...] = (own_ref[...] + dot(mix_halo, edges)).astype(BF16).astype(F32)
    keep = iota((MINOR, length), 1) >= iota((MINOR, length), 0)
    for c in range(0, rows, 2):
        pair = []
        for r in (c, c + 1):
            wide = jnp.broadcast_to(own_ref[r : r + 1, :], (MINOR, length))
            wide = pltpu.roll(wide, 0, 1, stride=1, stride_axis=0)
            pair.append(jnp.where(keep, wide, 0.0))
        shifted_ref[c * MINOR : (c + 2) * MINOR, :] = jnp.concatenate(pair, axis=0).astype(BF16)

    @pl.when(has_next)
    def _():
        to_next.wait_send()

    @pl.when(has_prev)
    def _():
        to_prev.wait_send()

    for copy in copies:
        copy.wait()


def correlate_kernel(per, gathered_ref, shifted_ref, out_ref, weights, blocks, sems):
    chans, _, packet = gathered_ref.shape
    length = shifted_ref.shape[1]
    middle = packet - length
    rows, lags, total = out_ref.shape
    lanes = pl.cdiv(total, LANES) * LANES
    packets = [gathered_ref[j].astype(F32) for j in range(chans)]
    packets = jnp.concatenate(packets, axis=0).astype(BF16)
    row, col = iota((total, chans * SLOT), 0), iota((total, chans * SLOT), 1)
    inside = jnp.bitwise_and(col, SLOT - 1)
    rank = row - (lax.shift_right_logical(col, SLOT.bit_length() - 1)) * per - inside
    early = inside < SLOT // 2

    def choose(chosen):
        return jnp.where(chosen, 1.0, 0.0).astype(BF16)

    whole = choose(rank == 0)
    halves = [
        choose(jnp.logical_and(rank == SLOT, early)),
        choose(jnp.logical_and(rank == SLOT // 2, jnp.logical_not(early))),
    ]
    sources = jnp.concatenate(
        [
            dot(whole, packets[:, h * middle : (h + 1) * middle])
            + dot(halves[h], packets[:, length:packet])
            for h in range(2)
        ],
        axis=1,
    )
    edge = iota((total, LANES), 1)
    scale = 1.0 / length**0.5
    if lanes > total:
        for h in range(2):
            fill = jnp.zeros((weights.shape[0], lanes - total, length), BF16)
            weights[:, h * lanes + total : (h + 1) * lanes, :] = fill
    copies = []
    for k in range(lags // (2 * MINOR)):
        for h in range(2):
            shift = (2 * k + h) * MINOR
            moved = sources
            if shift:
                moved = pltpu.roll(sources, length - shift, 1)
                tail = jnp.where(edge < LANES - shift, moved[:, length - LANES :], 0.0)
                moved = jnp.concatenate([moved[:, : length - LANES], tail], axis=1)
            weights[k, h * lanes : h * lanes + total, :] = moved.astype(BF16)
        result = dot(shifted_ref[...], weights[k], ((1,), (1,))) * scale
        low = result[:, 0:total].reshape(rows, MINOR, total)
        high = result[:, lanes : lanes + total].reshape(rows, MINOR, total)
        blocks[k] = jnp.concatenate([low, high], axis=1).astype(BF16)
        copy = pltpu.make_async_copy(
            blocks.at[k], out_ref.at[:, k * 2 * MINOR : (k + 1) * 2 * MINOR, :], sems.at[k]
        )
        copy.start()
        copies.append(copy)
    for copy in copies:
        copy.wait()


def shards(sections, chans, raw_traces, fir_taps, space_taps, source_index):
    rows, length = raw_traces.shape
    half = (space_taps.shape[0] - 1) // 2
    per = source_index.shape[1]
    total = per * chans
    lanes = -(-total // LANES) * LANES
    steps = LAGS // (2 * MINOR)
    vmem, hbm = pl.BlockSpec(memory_space=pltpu.VMEM), pl.BlockSpec(memory_space=pltpu.HBM)
    gathered, shifted = pl.pallas_call(
        functools.partial(exchange_kernel, sections, chans),
        out_shape=(
            jax.ShapeDtypeStruct((chans, SLOT, length + length // 2), BF16),
            jax.ShapeDtypeStruct((rows * MINOR, length), BF16),
        ),
        in_specs=[hbm, hbm, hbm, hbm],
        out_specs=(vmem, vmem),
        scratch_shapes=[
            pltpu.SMEM(source_index.shape, jnp.int32),
            pltpu.SMEM(space_taps.shape, F32),
            pltpu.VMEM((1, fir_taps.shape[0]), BF16),
            pltpu.VMEM((rows, length), BF16),
            pltpu.VMEM((8, 2 * LANES), F32),
            pltpu.VMEM((rows, length), BF16),
            pltpu.VMEM((2 * half, length), BF16),
            pltpu.VMEM((rows, length), F32),
            pltpu.VMEM((2 * SLOT, length), F32),
            pltpu.SemaphoreType.DMA((4,)),
            pltpu.SemaphoreType.DMA((2,)),
            pltpu.SemaphoreType.DMA((2,)),
            pltpu.SemaphoreType.DMA((chans,)),
            pltpu.SemaphoreType.DMA((chans,)),
        ],
        compiler_params=pltpu.CompilerParams(
            collective_id=0, has_side_effects=True, vmem_limit_bytes=24 * 2**20
        ),
        name="exchange",
    )(
        *(
            pltpu.with_memory_space_constraint(x, pltpu.HBM)
            for x in (source_index, space_taps, fir_taps.reshape(1, -1), raw_traces)
        )
    )
    return pl.pallas_call(
        functools.partial(correlate_kernel, per),
        out_shape=jax.ShapeDtypeStruct((rows, LAGS, total), BF16),
        in_specs=[vmem, vmem],
        out_specs=pl.BlockSpec(memory_space=pl.ANY),
        scratch_shapes=[
            pltpu.VMEM((steps, 2 * lanes, length), BF16),
            pltpu.VMEM((steps, rows, 2 * MINOR, total), BF16),
            pltpu.SemaphoreType.DMA((steps,)),
        ],
        compiler_params=pltpu.CompilerParams(vmem_limit_bytes=40 * 2**20),
        name="correlate",
    )(gathered, shifted)


def solution(mesh):
    return jax.shard_map(
        functools.partial(shards, mesh.shape["section"], mesh.shape["chan"]),
        mesh=mesh,
        in_specs=(P(("section", "chan"), None), P(), P(), P("section", "chan")),
        out_specs=P(("section", "chan"), None, None),
        check_vma=False,
    )
```
